256 devices in a mesh: table: 16 (over z_lo, x, core), batch: 16 (over y, z_hi).
Axes of the slice: x: 4, y: 4, z: 8 (z_hi: 4, z_lo: 2; z = z_hi * 2 + z_lo), core: 2. Of those that a mesh axis runs over, the one named last changes fastest.
Arguments:
- emb_table: bfloat16 [65536, 256], P('table'), may hold values from -2 to 2
- feature_ids: int32 [512, 1024, 8], P('batch', 'table'), may hold values from 0 to 4095
- projection: bfloat16 [1024, 256], P('table'), may hold values from -0.1875 to 0.1875
- norm_gain: float32 [256], replicated, may hold values from 0.1 to 1.9
- gate_weight: bfloat16 [256, 512], replicated, may hold values from -0.375 to 0.375
- up_weight: bfloat16 [256, 512], replicated, may hold values from -0.375 to 0.375
- down_weight: bfloat16 [512, 256], replicated, may hold values from -0.25 to 0.25
- out_grad: bfloat16 [512, 1024, 256], P(('batch', 'table')), may hold values from -24 to 24
Outputs:
- block_out: bfloat16 [512, 1024, 256], P(('batch', 'table'))
- table_grad: float32 [65536, 256], P(('table', 'batch'))
- projection_grad: float32 [1024, 256], P('table')
- gain_grad: float32 [256], replicated
- gate_grad: float32 [256, 512], replicated
- up_grad: float32 [256, 512], replicated
- down_grad: float32 [512, 256], replicated
The draws below stay inside these ranges and needn't reach their ends.
Inputs may be any that keep to these rules, and one draw needn't show every extreme that they name: `feature_ids`: an id names a row of the table shard of the device that holds the feature's table.
All inputs are finite; a program needn't handle non-finite values.
Results may differ from the reference program's by a relative error of at most 0.035.
Values may be sent and summed in bfloat16 or wider, within the bound.
No kernel may reach another device: no remote copies, remote signals or barrier semaphores. Data moves between devices by JAX's collectives and lax.ppermute only.
A program may use at most 128 MiB of HBM per device.

```python
import math
import jax
import jax.numpy as jnp
import numpy as np
from jax import lax

D = 256
K = 256
F = 1024
H = 512
POOL = 8
ROWS_DEV = 4096
SAMP = 32
SAMPLES = 512
ROWS = 65536
N_TABLE = 16


def plant(values, rng, least, high):
    index_at = [jax.random.randint(jax.random.fold_in(rng, axis), (), 0, length) for axis, length in enumerate(values.shape)]
    longest = values.shape.index(max(values.shape))
    beside = index_at[:longest] + [(index_at[longest] + 1) % values.shape[longest]] + index_at[longest + 1:]
    return values.at[tuple(index_at)].set(least).at[tuple(beside)].set(high)


def strengthened(values, stream_key, source, target, shards_of, factor):
    def block_of(axis_at):
        return (jnp.arange(values.shape[axis_at]) // (values.shape[axis_at] // shards_of)).reshape((-1,) + (1,) * (values.ndim - 1 - axis_at))

    near = jax.random.permutation(stream_key, shards_of)[block_of(target)]
    second = (block_of(target) + shards_of // 2) % shards_of
    return jnp.where((block_of(source) == near) | (block_of(source) == second), factor * values, values)


def levels(own_key, extent, cuts, low, largest):
    factor_of = 1.0
    for axis_at, parts in cuts:
        heights = jax.random.uniform(jax.random.fold_in(jax.random.fold_in(own_key, 6), axis_at), (parts,), jnp.float32, low / len(cuts), largest / len(cuts))
        factor_of = factor_of * jnp.repeat(jnp.exp(heights), extent[axis_at] // parts).reshape((-1,) + (1,) * (len(extent) - 1 - axis_at))
    return factor_of


def rank_bounds(number_of, lean):
    loads = [(1 << 20) // math.isqrt(rank ** lean) + 1 for rank in range(1, number_of + 1)]
    scale = 1 + sum(loads) // (1 << 30)
    return np.cumsum(np.array([max(1, weight // scale) for weight in loads]))


def ranked(key, shape, amount, skew):
    table = rank_bounds(amount, skew)
    ticket = jax.random.randint(jax.random.fold_in(key, 1), shape, 0, int(table[amount - 1]))
    standing = jnp.searchsorted(jnp.asarray(table, jnp.int32), ticket, side="right")
    return jax.random.permutation(jax.random.fold_in(key, 2), amount)[standing].astype(jnp.int32)


def gaussian(own_key, extent, scale, most, cuts=(), held_as=jnp.bfloat16):
    array = scale * jax.random.normal(own_key, extent, jnp.float32)
    if cuts:
        array = array * levels(own_key, extent, cuts, -0.22, 0.18)
    return jnp.clip(array, -most, most).astype(held_as)


def noise_with(stream_key, extent, deviation, limit, cuts, heavy, kind=jnp.bfloat16):
    drawn = deviation * jax.random.normal(stream_key, extent, jnp.float32)
    if cuts:
        drawn = drawn * levels(stream_key, extent, cuts, -0.22, 0.18)
    return jnp.clip(strengthened(drawn, jax.random.fold_in(stream_key, 3), *heavy), -limit, limit).astype(kind)


def setup_inputs(seed: int = 0) -> dict:
    key_of = jax.random.split(jax.random.key(seed), 9)
    emb_table = gaussian(key_of[0], (ROWS, D), 0.35, 2.0, ((0, 16),))
    feature_ids = plant(ranked(key_of[1], (SAMPLES, F, POOL), ROWS_DEV, 2), jax.random.fold_in(key_of[1], 3), 0, ROWS_DEV - 1).astype(jnp.int32)
    projection = gaussian(key_of[2], (F, K), F ** -0.5, 0.1875, ((0, 16),))
    norm_gain = jnp.clip(1.0 + 0.18 * jax.random.normal(key_of[3], (K,), jnp.float32), 0.1, 1.9)
    gate_weight = gaussian(key_of[4], (K, H), K ** -0.5, 0.375)
    up_weight = gaussian(key_of[5], (K, H), K ** -0.5, 0.375)
    down_weight = gaussian(key_of[6], (H, D), H ** -0.5, 0.25)
    out_grad = noise_with(key_of[7], (SAMPLES, F, D), 1.0, 24.0, ((0, 256),), (0, 2, 256, 6.0))
    return dict(emb_table=emb_table, feature_ids=feature_ids, projection=projection, norm_gain=norm_gain, gate_weight=gate_weight, up_weight=up_weight, down_weight=down_weight, out_grad=out_grad)


epsilon = 1e-06

def mlp_forward(interact, norm_gain, gate_weight, up_weight, down_weight):
    mean_sq = lax.optimization_barrier(jnp.mean(interact * interact, axis=-1, keepdims=True))
    inv_rms = lax.rsqrt(mean_sq + epsilon)
    normed = interact * inv_rms
    scaled = (normed * norm_gain).astype(jnp.bfloat16)
    gate_pre = jnp.dot(scaled, gate_weight, preferred_element_type=jnp.float32)
    up_pre = jnp.dot(scaled, up_weight, preferred_element_type=jnp.float32)
    hidden = (jax.nn.silu(gate_pre) * up_pre).astype(jnp.bfloat16)
    result = jnp.dot(hidden, down_weight, preferred_element_type=jnp.float32).astype(jnp.bfloat16)
    return (result, (inv_rms, normed, scaled, gate_pre, up_pre, hidden))

def contract(left, right, left_dim, right_dim):
    return lax.dot_general(left, right, (((left_dim,), (right_dim,)), ((), ())), preferred_element_type=jnp.float32)

def mlp_backward(stored, grad_rows, norm_gain, gate_weight, up_weight, down_weight):
    inv_rms, normed, scaled, gate_pre, up_pre, hidden = stored
    hidden_grad = contract(grad_rows, down_weight, 1, 1)
    down_part = contract(hidden, grad_rows, 0, 0)
    sigmoid_gate = jax.nn.sigmoid(gate_pre)
    up_pre_grad = (hidden_grad * jax.nn.silu(gate_pre)).astype(jnp.bfloat16)
    gate_pre_grad = (hidden_grad * up_pre * sigmoid_gate * (1.0 + gate_pre * (1.0 - sigmoid_gate))).astype(jnp.bfloat16)
    gate_part = contract(scaled, gate_pre_grad, 0, 0)
    up_part = contract(scaled, up_pre_grad, 0, 0)
    scaled_grad = contract(gate_pre_grad, gate_weight, 1, 1) + contract(up_pre_grad, up_weight, 1, 1)
    gain_part = lax.optimization_barrier(jnp.sum(scaled_grad * normed, axis=0))
    inner_term = scaled_grad * norm_gain
    interact_grad = inv_rms * (inner_term - normed * lax.optimization_barrier(jnp.mean(inner_term * normed, axis=-1, keepdims=True)))
    return (interact_grad.astype(jnp.bfloat16), gate_part, up_part, down_part, gain_part)

def round_partial(values):
    return lax.optimization_barrier(values.astype(jnp.bfloat16)).astype(jnp.float32)

def reference(emb_table, feature_ids, projection, norm_gain, gate_weight, up_weight, down_weight, out_grad):
    shards = N_TABLE
    feat_here = F // N_TABLE
    blocks = SAMPLES // SAMP
    offsets = jnp.arange(F, dtype=jnp.int32) // feat_here * ROWS_DEV
    ids_blocks = feature_ids.reshape(blocks, SAMP, F, POOL)
    grad_blocks = out_grad.reshape(blocks, SAMP, F, D)
    proj_wide = projection.astype(jnp.float32)
    proj_shards = proj_wide.reshape(shards, feat_here, K)
    totals = (jnp.zeros((ROWS, D), jnp.float32), jnp.zeros((F, K), jnp.float32), jnp.zeros((K, H), jnp.float32), jnp.zeros((K, H), jnp.float32), jnp.zeros((H, D), jnp.float32), jnp.zeros((K,), jnp.float32))

    def block_step(sums, inputs):
        block_ids, block_grad = inputs
        row_ids = (block_ids + offsets[None, :, None]).astype(jnp.int32)
        embeds = lax.optimization_barrier(jnp.sum(emb_table[row_ids].astype(jnp.float32), axis=2)).astype(jnp.bfloat16)
        embeds_wide = embeds.astype(jnp.float32)
        emb_shards = embeds_wide.reshape(SAMP, shards, feat_here, D)
        z_partial = round_partial(jnp.einsum('stfd,tfk->stdk', emb_shards, proj_shards))
        inter_map = lax.optimization_barrier(jnp.sum(z_partial, axis=1)).astype(jnp.bfloat16)
        inter_wide = inter_map.astype(jnp.float32)
        interact = jnp.einsum('sfd,sdk->sfk', embeds_wide, inter_wide)
        result, stored = mlp_forward(interact.reshape(SAMP * F, K), norm_gain, gate_weight, up_weight, down_weight)
        interact_grad, gate_part, up_part, down_part, gain_part = mlp_backward(stored, block_grad.reshape(SAMP * F, D), norm_gain, gate_weight, up_weight, down_weight)
        igrad_wide = interact_grad.astype(jnp.float32).reshape(SAMP, F, K)
        zgrad_partial = round_partial(jnp.einsum('stfd,stfk->stdk', emb_shards, igrad_wide.reshape(SAMP, shards, feat_here, K)))
        inter_grad = lax.optimization_barrier(jnp.sum(zgrad_partial, axis=1)).astype(jnp.bfloat16)
        igrad_map = inter_grad.astype(jnp.float32)
        embed_grad = (jnp.einsum('sfk,sdk->sfd', igrad_wide, inter_wide) + jnp.einsum('fk,sdk->sfd', proj_wide, igrad_map)).astype(jnp.bfloat16)
        spread = jnp.broadcast_to(embed_grad.astype(jnp.float32)[:, :, None, :], (SAMP, F, POOL, D))
        table_sum = sums[0] + jax.ops.segment_sum(spread.reshape(-1, D), row_ids.reshape(-1), num_segments=ROWS)
        proj_sum = sums[1] + jnp.einsum('sfd,sdk->fk', embeds_wide, igrad_map)
        updated = (table_sum, proj_sum, sums[2] + gate_part, sums[3] + up_part, sums[4] + down_part, sums[5] + gain_part)
        return (updated, result.reshape(SAMP, F, D))
    sums, outputs = lax.scan(block_step, totals, (ids_blocks, grad_blocks))
    block_out = outputs.reshape(SAMPLES, F, D)
    return (block_out, sums[0], sums[1], sums[5], sums[2], sums[3], sums[4])
```

```python
import jax
import jax.numpy as jnp
from jax import lax
from jax.experimental import pallas as pl
from jax.experimental.pallas import tpu as pltpu
from jax.sharding import PartitionSpec as P

epsilon = 1e-06
BF = jnp.bfloat16
F32 = jnp.float32
Y_GROUPS = [[z + 4 * y for y in range(4)] for z in range(4)]
Z_GROUPS = [[4 * y + z for z in range(4)] for y in range(4)]


def contract(left, right, left_dim, right_dim):
    return lax.dot_general(
        left, right, (((left_dim,), (right_dim,)), ((), ())), preferred_element_type=F32
    )


def lookup_kernel(high_ref, low_ref, table_ref, counts_ref, embeds_ref):
    groups = high_ref.shape[0]
    place = lax.broadcasted_iota(jnp.int32, (256, 128), 0)

    def step(g, carry):
        left = jnp.where(place == high_ref[pl.ds(g, 1), :], 1.0, 0.0).astype(BF)
        right = jnp.where(place == low_ref[pl.ds(g, 1), :], 1.0, 0.0).astype(BF)
        both = contract(left, right, 1, 1).astype(BF)
        for h in range(16):
            counts_ref[pl.ds(pl.multiple_of(g * 16, 16), 16), h * 256 : (h + 1) * 256] = both[
                h * 16 : (h + 1) * 16
            ]
        return carry

    lax.fori_loop(0, groups, step, 0, unroll=2)
    embeds_ref[...] = jnp.dot(
        counts_ref[...], table_ref[...], preferred_element_type=F32
    ).astype(BF)


def lookup(emb_table, feature_ids):
    samples, feats, pool = feature_ids.shape
    rows = samples * feats
    lanes = (
        feature_ids.reshape(samples, feats // 16, 16, pool)
        .transpose(0, 1, 3, 2)
        .reshape(rows // 16, 128)
    )
    high = (lanes // 256) * 16 + lax.broadcasted_iota(jnp.int32, lanes.shape, 1) % 16
    low = lanes % 256
    steps = 4
    return pl.pallas_call(
        lookup_kernel,
        grid=(steps,),
        in_specs=[
            pl.BlockSpec((rows // 16 // steps, 128), lambda i: (i, 0)),
            pl.BlockSpec((rows // 16 // steps, 128), lambda i: (i, 0)),
            pl.BlockSpec(emb_table.shape, lambda i: (0, 0)),
        ],
        out_specs=[
            pl.BlockSpec((rows // steps, emb_table.shape[0]), lambda i: (i, 0)),
            pl.BlockSpec((rows // steps, emb_table.shape[1]), lambda i: (i, 0)),
        ],
        out_shape=[
            jax.ShapeDtypeStruct((rows, emb_table.shape[0]), BF),
            jax.ShapeDtypeStruct((rows, emb_table.shape[1]), BF),
        ],
        name="lookup",
    )(high, low, emb_table)


def exchange(values, axis, groups=None):
    return lax.all_to_all(values, axis, 0, 0, axis_index_groups=groups)


def gathered(values, axis, size):
    return exchange(jnp.broadcast_to(values[None], (size,) + values.shape), axis)


def mlp_forward(interact, norm_gain, gate_weight, up_weight, down_weight):
    mean_sq = jnp.mean(interact * interact, axis=-1, keepdims=True)
    inv_rms = lax.rsqrt(mean_sq + epsilon)
    normed = interact * inv_rms
    scaled = (normed * norm_gain).astype(BF)
    gate_pre = jnp.dot(scaled, gate_weight, preferred_element_type=F32)
    up_pre = jnp.dot(scaled, up_weight, preferred_element_type=F32)
    hidden = (jax.nn.silu(gate_pre) * up_pre).astype(BF)
    result = jnp.dot(hidden, down_weight, preferred_element_type=F32).astype(BF)
    return (result, (inv_rms, normed, scaled, gate_pre, up_pre, hidden))


def mlp_backward(stored, grad_rows, norm_gain, gate_weight, up_weight, down_weight):
    inv_rms, normed, scaled, gate_pre, up_pre, hidden = stored
    hidden_grad = contract(grad_rows, down_weight, 1, 1)
    down_part = contract(hidden, grad_rows, 0, 0)
    sigmoid_gate = jax.nn.sigmoid(gate_pre)
    up_pre_grad = (hidden_grad * jax.nn.silu(gate_pre)).astype(BF)
    gate_pre_grad = (
        hidden_grad * up_pre * sigmoid_gate * (1.0 + gate_pre * (1.0 - sigmoid_gate))
    ).astype(BF)
    gate_part = contract(scaled, gate_pre_grad, 0, 0)
    up_part = contract(scaled, up_pre_grad, 0, 0)
    scaled_grad = contract(gate_pre_grad, gate_weight, 1, 1) + contract(
        up_pre_grad, up_weight, 1, 1
    )
    gain_part = jnp.sum(scaled_grad * normed, axis=0)
    inner_term = scaled_grad * norm_gain
    interact_grad = inv_rms * (
        inner_term - normed * jnp.mean(inner_term * normed, axis=-1, keepdims=True)
    )
    return (interact_grad.astype(BF), gate_part, up_part, down_part, gain_part)


def per_device(
    emb_table, feature_ids, projection, norm_gain, gate_weight, up_weight, down_weight, out_grad
):
    samples, feats, _ = feature_ids.shape
    shards = 16
    own = samples // shards
    width = emb_table.shape[1]
    rank = projection.shape[1]
    all_feats = shards * feats
    proj = gathered(projection, "table", shards).reshape(all_feats, rank)
    counts, embeds = lookup(emb_table, feature_ids)
    x = (
        exchange(embeds.reshape(shards, own, feats, width), "table")
        .transpose(1, 0, 2, 3)
        .reshape(own, all_feats, width)
    )
    inter_map = jnp.einsum("sfd,fk->sdk", x, proj, preferred_element_type=F32).astype(BF)
    interact = jnp.einsum("sfd,sdk->sfk", x, inter_map, preferred_element_type=F32)
    result, stored = mlp_forward(
        interact.reshape(-1, rank), norm_gain, gate_weight, up_weight, down_weight
    )
    block_out = result.reshape(own, all_feats, width)
    interact_grad, gate_part, up_part, down_part, gain_part = mlp_backward(
        stored, out_grad.reshape(-1, width), norm_gain, gate_weight, up_weight, down_weight
    )
    interact_grad = interact_grad.reshape(own, all_feats, rank)
    inter_grad = jnp.einsum("sfd,sfk->sdk", x, interact_grad, preferred_element_type=F32).astype(
        BF
    )
    embed_grad = (
        jnp.einsum("sfk,sdk->sfd", interact_grad, inter_map, preferred_element_type=F32)
        + jnp.einsum("fk,sdk->sfd", proj, inter_grad, preferred_element_type=F32)
    ).astype(BF)
    back = exchange(
        embed_grad.reshape(own, shards, feats, width).transpose(1, 0, 2, 3), "table"
    ).reshape(-1, width)

    proj_part = jnp.einsum("sfd,sdk->fk", x, inter_grad, preferred_element_type=F32)
    hidden_width = gate_part.shape[1]

    def halves(part):
        return (
            part.astype(BF)
            .reshape(shards, rank // shards, 2, hidden_width // 2)
            .transpose(0, 2, 1, 3)
            .reshape(shards, -1, width)
        )

    gain_rows = jnp.pad(gain_part.astype(BF)[None], ((0, 15), (0, 0)))
    parts = jnp.concatenate(
        [
            halves(gate_part),
            halves(up_part),
            down_part.astype(BF).reshape(shards, -1, width),
            proj_part.astype(BF).reshape(shards, -1, width),
            jnp.broadcast_to(gain_rows[None], (shards, 16, width)),
        ],
        axis=1,
    )
    parts = jnp.sum(exchange(parts, "table").astype(F32), axis=0).astype(BF)
    rows = parts.shape[0]
    parts = exchange(parts.reshape(16, rows // 16, width), "batch")
    parts = jnp.sum(parts.astype(F32), axis=0).astype(BF)
    parts = gathered(parts, "batch", 16).reshape(rows, width)
    projection_grad = parts[96:160].astype(F32)
    gain_grad = parts[160].astype(F32)
    weights = gathered(parts[:96], "table", shards).astype(F32)

    def joined(piece):
        return (
            piece.reshape(shards, 2, rank // shards, hidden_width // 2)
            .transpose(0, 2, 1, 3)
            .reshape(rank, hidden_width)
        )

    gate_grad = joined(weights[:, :32])
    up_grad = joined(weights[:, 32:64])
    down_grad = weights[:, 64:96].reshape(hidden_width, width)

    table_term = contract(counts, back, 0, 0).astype(BF)
    here = table_term.shape[0] // 16
    table_term = exchange(table_term.reshape(4, 4 * here, width), "batch", Y_GROUPS)
    table_term = jnp.sum(table_term.astype(F32), axis=0).astype(BF)
    table_term = exchange(table_term.reshape(4, here, width), "batch", Z_GROUPS)
    table_grad = jnp.sum(table_term.astype(F32), axis=0)
    return (block_out, table_grad, projection_grad, gain_grad, gate_grad, up_grad, down_grad)


def solution(mesh):
    return jax.shard_map(
        per_device,
        mesh=mesh,
        in_specs=(
            P("table", None),
            P("batch", "table", None),
            P("table", None),
            P(),
            P(),
            P(),
            P(),
            P(("batch", "table"), None, None),
        ),
        out_specs=(
            P(("batch", "table"), None, None),
            P(("table", "batch"), None),
            P("table", None),
            P(),
            P(),
            P(),
            P(),
        ),
        check_vma=False,
    )
```

```python
import jax
import jax.numpy as jnp
from jax import lax
from jax.experimental import pallas as pl
from jax.sharding import PartitionSpec as P

epsilon = 1e-06
BF = jnp.bfloat16
F32 = jnp.float32
STEPS = {"y": 4, "z": 1}


def contract(left, right, left_dim, right_dim):
    return lax.dot_general(
        left, right, (((left_dim,), (right_dim,)), ((), ())), preferred_element_type=F32
    )


def lookup_kernel(high_ref, low_ref, table_ref, counts_ref, embeds_ref):
    groups = high_ref.shape[0]
    slot = lax.broadcasted_iota(jnp.int32, (256, 128), 0)

    def step(g, carry):
        left = jnp.where(slot == high_ref[pl.ds(g, 1), :], 1.0, 0.0).astype(BF)
        right = jnp.where(slot == low_ref[pl.ds(g, 1), :], 1.0, 0.0).astype(BF)
        both = contract(left, right, 1, 1).astype(BF)
        for h in range(16):
            counts_ref[pl.ds(pl.multiple_of(g * 16, 16), 16), h * 256 : (h + 1) * 256] = both[
                h * 16 : (h + 1) * 16
            ]
        return carry

    lax.fori_loop(0, groups, step, 0, unroll=2)
    embeds_ref[...] = jnp.dot(
        counts_ref[...], table_ref[...], preferred_element_type=F32
    ).astype(BF)


def lookup(emb_table, feature_ids):
    samples, feats, pool = feature_ids.shape
    rows = samples * feats
    lanes = (
        feature_ids.reshape(samples, feats // 16, 16, pool)
        .transpose(0, 1, 3, 2)
        .reshape(rows // 16, 128)
    )
    high = (lanes // 256) * 16 + lax.broadcasted_iota(jnp.int32, lanes.shape, 1) % 16
    low = lanes % 256
    steps = 4
    return pl.pallas_call(
        lookup_kernel,
        grid=(steps,),
        in_specs=[
            pl.BlockSpec((rows // 16 // steps, 128), lambda i: (i, 0)),
            pl.BlockSpec((rows // 16 // steps, 128), lambda i: (i, 0)),
            pl.BlockSpec(emb_table.shape, lambda i: (0, 0)),
        ],
        out_specs=[
            pl.BlockSpec((rows // steps, emb_table.shape[0]), lambda i: (i, 0)),
            pl.BlockSpec((rows // steps, emb_table.shape[1]), lambda i: (i, 0)),
        ],
        out_shape=[
            jax.ShapeDtypeStruct((rows, emb_table.shape[0]), BF),
            jax.ShapeDtypeStruct((rows, emb_table.shape[1]), BF),
        ],
        cost_estimate=pl.CostEstimate(
            flops=4 * rows * emb_table.shape[0] * emb_table.shape[1],
            bytes_accessed=2 * rows * emb_table.shape[0] + 4 * emb_table.size,
            transcendentals=0,
        ),
        name="lookup",
    )(high, low, emb_table)


def exchange(values, axis):
    return lax.all_to_all(values, axis, 0, 0)


def place(part):
    batch = lax.axis_index("batch")
    return batch // 4 if part == "y" else batch % 4


def swap(values, part, offset):
    pairs = [(b, b ^ (STEPS[part] * offset)) for b in range(16)]
    return lax.ppermute(values, "batch", pairs)


def sum_scattered(values, part):
    mine = place(part)
    take = lambda i: lax.dynamic_index_in_dim(values, i, 0, keepdims=False)
    came = [swap(take(mine ^ k), part, k) for k in (1, 2, 3)]
    return sum((c.astype(F32) for c in came), take(mine).astype(F32))


def sum_all(values, part):
    came = [swap(values, part, k) for k in (1, 2, 3)]
    return sum((c.astype(F32) for c in came), values.astype(F32)).astype(BF)


def gathered(values, axis, size):
    return exchange(jnp.broadcast_to(values[None], (size,) + values.shape), axis)


def mlp_forward(interact, norm_gain, gate_weight, up_weight, down_weight):
    mean_sq = jnp.mean(interact * interact, axis=-1, keepdims=True)
    inv_rms = lax.rsqrt(mean_sq + epsilon)
    normed = interact * inv_rms
    scaled = (normed * norm_gain).astype(BF)
    gate_pre = jnp.dot(scaled, gate_weight, preferred_element_type=F32)
    up_pre = jnp.dot(scaled, up_weight, preferred_element_type=F32)
    hidden = (jax.nn.silu(gate_pre) * up_pre).astype(BF)
    result = jnp.dot(hidden, down_weight, preferred_element_type=F32).astype(BF)
    return (result, (inv_rms, normed, scaled, gate_pre, up_pre, hidden))


def mlp_backward(stored, grad_rows, norm_gain, gate_weight, up_weight, down_weight):
    inv_rms, normed, scaled, gate_pre, up_pre, hidden = stored
    hidden_grad = contract(grad_rows, down_weight, 1, 1)
    down_part = contract(hidden, grad_rows, 0, 0)
    sigmoid_gate = jax.nn.sigmoid(gate_pre)
    up_pre_grad = (hidden_grad * jax.nn.silu(gate_pre)).astype(BF)
    gate_pre_grad = (
        hidden_grad * up_pre * sigmoid_gate * (1.0 + gate_pre * (1.0 - sigmoid_gate))
    ).astype(BF)
    gate_part = contract(scaled, gate_pre_grad, 0, 0)
    up_part = contract(scaled, up_pre_grad, 0, 0)
    scaled_grad = contract(gate_pre_grad, gate_weight, 1, 1) + contract(
        up_pre_grad, up_weight, 1, 1
    )
    gain_part = jnp.sum(scaled_grad * normed, axis=0)
    inner_term = scaled_grad * norm_gain
    interact_grad = inv_rms * (
        inner_term - normed * jnp.mean(inner_term * normed, axis=-1, keepdims=True)
    )
    return (interact_grad.astype(BF), gate_part, up_part, down_part, gain_part)


def per_device(
    emb_table, feature_ids, projection, norm_gain, gate_weight, up_weight, down_weight, out_grad
):
    samples, feats, _ = feature_ids.shape
    shards = 16
    own = samples // shards
    width = emb_table.shape[1]
    rank = projection.shape[1]
    all_feats = shards * feats
    proj = gathered(projection, "table", shards).reshape(all_feats, rank)
    counts, embeds = lookup(emb_table, feature_ids)
    embeds, proj = lax.optimization_barrier((embeds, proj))
    x = (
        exchange(embeds.reshape(shards, own, feats, width), "table")
        .transpose(1, 0, 2, 3)
        .reshape(own, all_feats, width)
    )
    inter_map = jnp.einsum("sfd,fk->sdk", x, proj, preferred_element_type=F32).astype(BF)
    interact = jnp.einsum("sfd,sdk->sfk", x, inter_map, preferred_element_type=F32)
    result, stored = mlp_forward(
        interact.reshape(-1, rank), norm_gain, gate_weight, up_weight, down_weight
    )
    block_out = result.reshape(own, all_feats, width)
    interact_grad, gate_part, up_part, down_part, gain_part = mlp_backward(
        stored, out_grad.reshape(-1, width), norm_gain, gate_weight, up_weight, down_weight
    )
    interact_grad = interact_grad.reshape(own, all_feats, rank)
    inter_grad = jnp.einsum("sfd,sfk->sdk", x, interact_grad, preferred_element_type=F32).astype(
        BF
    )
    embed_grad = (
        jnp.einsum("sfk,sdk->sfd", interact_grad, inter_map, preferred_element_type=F32)
        + jnp.einsum("fk,sdk->sfd", proj, inter_grad, preferred_element_type=F32)
    ).astype(BF)
    back = exchange(
        embed_grad.reshape(own, shards, feats, width).transpose(1, 0, 2, 3), "table"
    ).reshape(-1, width)

    proj_part = jnp.einsum("sfd,sdk->fk", x, inter_grad, preferred_element_type=F32)
    hidden_width = gate_part.shape[1]

    def halves(part):
        return (
            part.astype(BF)
            .reshape(shards, rank // shards, 2, hidden_width // 2)
            .transpose(0, 2, 1, 3)
            .reshape(shards, -1, width)
        )

    gain_rows = jnp.pad(gain_part.astype(BF)[None], ((0, 15), (0, 0)))
    parts = jnp.concatenate(
        [
            halves(gate_part),
            halves(up_part),
            down_part.astype(BF).reshape(shards, -1, width),
            proj_part.astype(BF).reshape(shards, -1, width),
            jnp.broadcast_to(gain_rows[None], (shards, 16, width)),
        ],
        axis=1,
    )
    parts, back = lax.optimization_barrier((parts, back))
    parts = exchange(parts, "table")
    parts = jnp.sum(parts.astype(F32), axis=0).astype(BF)
    parts = sum_all(sum_all(parts, "y"), "z")
    projection_grad = parts[96:160].astype(F32)
    gain_grad = parts[160].astype(F32)
    weights = gathered(parts[:96], "table", shards).astype(F32)

    def joined(piece):
        return (
            piece.reshape(shards, 2, rank // shards, hidden_width // 2)
            .transpose(0, 2, 1, 3)
            .reshape(rank, hidden_width)
        )

    gate_grad = joined(weights[:, :32])
    up_grad = joined(weights[:, 32:64])
    down_grad = weights[:, 64:96].reshape(hidden_width, width)

    table_term = contract(counts, back, 0, 0).astype(BF)
    here = table_term.shape[0] // 16
    table_term = sum_scattered(table_term.reshape(4, 4 * here, width), "y").astype(BF)
    table_grad = sum_scattered(table_term.reshape(4, here, width), "z")
    return (block_out, table_grad, projection_grad, gain_grad, gate_grad, up_grad, down_grad)


def solution(mesh):
    return jax.shard_map(
        per_device,
        mesh=mesh,
        in_specs=(
            P("table", None),
            P("batch", "table", None),
            P("table", None),
            P(),
            P(),
            P(),
            P(),
            P(("batch", "table"), None, None),
        ),
        out_specs=(
            P(("batch", "table"), None, None),
            P(("table", "batch"), None),
            P("table", None),
            P(),
            P(),
            P(),
            P(),
        ),
        check_vma=False,
    )
```

```python
import jax
import jax.numpy as jnp
from jax import lax
from jax.experimental import pallas as pl
from jax.sharding import PartitionSpec as P

epsilon = 1e-06
BF = jnp.bfloat16
F32 = jnp.float32
STEPS = {"y": 4, "z": 1}


def contract(left, right, left_dim, right_dim):
    return lax.dot_general(
        left, right, (((left_dim,), (right_dim,)), ((), ())), preferred_element_type=F32
    )


def lookup_kernel(high_ref, low_ref, table_ref, counts_ref, embeds_ref):
    groups = high_ref.shape[0]
    slot = lax.broadcasted_iota(jnp.int32, (256, 128), 0)

    def step(g, carry):
        left = jnp.where(slot == high_ref[pl.ds(g, 1), :], 1.0, 0.0).astype(BF)
        right = jnp.where(slot == low_ref[pl.ds(g, 1), :], 1.0, 0.0).astype(BF)
        both = contract(left, right, 1, 1).astype(BF)
        for h in range(16):
            counts_ref[pl.ds(pl.multiple_of(g * 16, 16), 16), h * 256 : (h + 1) * 256] = both[
                h * 16 : (h + 1) * 16
            ]
        return carry

    lax.fori_loop(0, groups, step, 0, unroll=8)
    embeds_ref[...] = jnp.dot(
        counts_ref[...], table_ref[...], preferred_element_type=F32
    ).astype(BF)


def lookup(emb_table, feature_ids):
    samples, feats, pool = feature_ids.shape
    rows = samples * feats
    lanes = (
        feature_ids.reshape(samples, feats // 16, 16, pool)
        .transpose(0, 1, 3, 2)
        .reshape(rows // 16, 128)
    )
    high = (lanes // 256) * 16 + lax.broadcasted_iota(jnp.int32, lanes.shape, 1) % 16
    low = lanes % 256
    steps = 4
    return pl.pallas_call(
        lookup_kernel,
        grid=(steps,),
        in_specs=[
            pl.BlockSpec((rows // 16 // steps, 128), lambda i: (i, 0)),
            pl.BlockSpec((rows // 16 // steps, 128), lambda i: (i, 0)),
            pl.BlockSpec(emb_table.shape, lambda i: (0, 0)),
        ],
        out_specs=[
            pl.BlockSpec((rows // steps, emb_table.shape[0]), lambda i: (i, 0)),
            pl.BlockSpec((rows // steps, emb_table.shape[1]), lambda i: (i, 0)),
        ],
        out_shape=[
            jax.ShapeDtypeStruct((rows, emb_table.shape[0]), BF),
            jax.ShapeDtypeStruct((rows, emb_table.shape[1]), BF),
        ],
        cost_estimate=pl.CostEstimate(
            flops=4 * rows * emb_table.shape[0] * emb_table.shape[1],
            bytes_accessed=2 * rows * emb_table.shape[0] + 4 * emb_table.size,
            transcendentals=0,
        ),
        name="lookup",
    )(high, low, emb_table)


def exchange(values, axis):
    return lax.all_to_all(values, axis, 0, 0)


def place(part):
    batch = lax.axis_index("batch")
    return batch // 4 if part == "y" else batch % 4


def swap(values, part, offset):
    pairs = [(b, b ^ (STEPS[part] * offset)) for b in range(16)]
    return lax.ppermute(values, "batch", pairs)


def sum_scattered(values, part):
    mine = place(part)
    take = lambda i: lax.dynamic_index_in_dim(values, i, 0, keepdims=False)
    came = [swap(take(mine ^ k), part, k) for k in (1, 2, 3)]
    return sum((c.astype(F32) for c in came), take(mine).astype(F32))


def sum_all(values, part):
    came = [swap(values, part, k) for k in (1, 2, 3)]
    return sum((c.astype(F32) for c in came), values.astype(F32)).astype(BF)


def gathered(values, axis, size):
    return exchange(jnp.broadcast_to(values[None], (size,) + values.shape), axis)


def mlp_forward(interact, norm_gain, gate_weight, up_weight, down_weight):
    mean_sq = jnp.mean(interact * interact, axis=-1, keepdims=True)
    inv_rms = lax.rsqrt(mean_sq + epsilon)
    normed = interact * inv_rms
    scaled = (normed * norm_gain).astype(BF)
    gate_pre = jnp.dot(scaled, gate_weight, preferred_element_type=F32)
    up_pre = jnp.dot(scaled, up_weight, preferred_element_type=F32)
    hidden = (jax.nn.silu(gate_pre) * up_pre).astype(BF)
    result = jnp.dot(hidden, down_weight, preferred_element_type=F32).astype(BF)
    return (result, (inv_rms, normed, scaled, gate_pre, up_pre, hidden))


def mlp_backward(stored, grad_rows, norm_gain, gate_weight, up_weight, down_weight):
    inv_rms, normed, scaled, gate_pre, up_pre, hidden = stored
    hidden_grad = contract(grad_rows, down_weight, 1, 1)
    down_part = contract(hidden, grad_rows, 0, 0)
    sigmoid_gate = jax.nn.sigmoid(gate_pre)
    up_pre_grad = (hidden_grad * jax.nn.silu(gate_pre)).astype(BF)
    gate_pre_grad = (
        hidden_grad * up_pre * sigmoid_gate * (1.0 + gate_pre * (1.0 - sigmoid_gate))
    ).astype(BF)
    gate_part = contract(scaled, gate_pre_grad, 0, 0)
    up_part = contract(scaled, up_pre_grad, 0, 0)
    scaled_grad = contract(gate_pre_grad, gate_weight, 1, 1) + contract(
        up_pre_grad, up_weight, 1, 1
    )
    gain_part = jnp.sum(scaled_grad * normed, axis=0)
    inner_term = scaled_grad * norm_gain
    interact_grad = inv_rms * (
        inner_term - normed * jnp.mean(inner_term * normed, axis=-1, keepdims=True)
    )
    return (interact_grad.astype(BF), gate_part, up_part, down_part, gain_part)


def per_device(
    emb_table, feature_ids, projection, norm_gain, gate_weight, up_weight, down_weight, out_grad
):
    samples, feats, _ = feature_ids.shape
    shards = 16
    own = samples // shards
    width = emb_table.shape[1]
    rank = projection.shape[1]
    all_feats = shards * feats
    proj = gathered(projection, "table", shards).reshape(all_feats, rank)
    counts, embeds = lookup(emb_table, feature_ids)
    embeds, proj = lax.optimization_barrier((embeds, proj))
    x = (
        exchange(embeds.reshape(shards, own, feats, width), "table")
        .transpose(1, 0, 2, 3)
        .reshape(own, all_feats, width)
    )
    inter_map = jnp.einsum("sfd,fk->sdk", x, proj, preferred_element_type=F32).astype(BF)
    interact = jnp.einsum("sfd,sdk->sfk", x, inter_map, preferred_element_type=F32)
    result, stored = mlp_forward(
        interact.reshape(-1, rank), norm_gain, gate_weight, up_weight, down_weight
    )
    block_out = result.reshape(own, all_feats, width)
    interact_grad, gate_part, up_part, down_part, gain_part = mlp_backward(
        stored, out_grad.reshape(-1, width), norm_gain, gate_weight, up_weight, down_weight
    )
    interact_grad = interact_grad.reshape(own, all_feats, rank)
    inter_grad = jnp.einsum("sfd,sfk->sdk", x, interact_grad, preferred_element_type=F32).astype(
        BF
    )
    embed_grad = (
        jnp.einsum("sfk,sdk->sfd", interact_grad, inter_map, preferred_element_type=F32)
        + jnp.einsum("fk,sdk->sfd", proj, inter_grad, preferred_element_type=F32)
    ).astype(BF)
    back = exchange(
        embed_grad.reshape(own, shards, feats, width).transpose(1, 0, 2, 3), "table"
    ).reshape(-1, width)

    proj_part = jnp.einsum("sfd,sdk->fk", x, inter_grad, preferred_element_type=F32)
    hidden_width = gate_part.shape[1]

    def halves(part):
        return (
            part.astype(BF)
            .reshape(shards, rank // shards, 2, hidden_width // 2)
            .transpose(0, 2, 1, 3)
            .reshape(shards, -1, width)
        )

    gain_rows = jnp.pad(gain_part.astype(BF)[None], ((0, 15), (0, 0)))
    parts = jnp.concatenate(
        [
            halves(gate_part),
            halves(up_part),
            down_part.astype(BF).reshape(shards, -1, width),
            proj_part.astype(BF).reshape(shards, -1, width),
            jnp.broadcast_to(gain_rows[None], (shards, 16, width)),
        ],
        axis=1,
    )
    parts, back = lax.optimization_barrier((parts, back))
    parts = exchange(parts, "table")
    parts = jnp.sum(parts.astype(F32), axis=0).astype(BF)
    parts = sum_all(parts, "z")
    parts = sum_all(parts, "y")
    projection_grad = parts[96:160].astype(F32)
    gain_grad = parts[160].astype(F32)
    weights = gathered(parts[:96], "table", shards)
    weights = weights.astype(F32)

    def joined(piece):
        return (
            piece.reshape(shards, 2, rank // shards, hidden_width // 2)
            .transpose(0, 2, 1, 3)
            .reshape(rank, hidden_width)
        )

    gate_grad = joined(weights[:, :32])
    up_grad = joined(weights[:, 32:64])
    down_grad = weights[:, 64:96].reshape(hidden_width, width)

    table_term = contract(counts, back, 0, 0).astype(BF)
    here = table_term.shape[0] // 16
    table_term = sum_scattered(table_term.reshape(4, 4 * here, width), "y").astype(BF)
    table_grad = sum_scattered(table_term.reshape(4, here, width), "z")
    return (block_out, table_grad, projection_grad, gain_grad, gate_grad, up_grad, down_grad)


def solution(mesh):
    return jax.shard_map(
        per_device,
        mesh=mesh,
        in_specs=(
            P("table", None),
            P("batch", "table", None),
            P("table", None),
            P(),
            P(),
            P(),
            P(),
            P(("batch", "table"), None, None),
        ),
        out_specs=(
            P(("batch", "table"), None, None),
            P(("table", "batch"), None),
            P("table", None),
            P(),
            P(),
            P(),
            P(),
        ),
        check_vma=False,
    )
```

```python
import functools

import jax
import jax.numpy as jnp
from jax import lax
from jax.experimental import pallas as pl
from jax.experimental.pallas import tpu as pltpu
from jax.sharding import PartitionSpec as P

epsilon = 1e-06
BF = jnp.bfloat16
F32 = jnp.float32
STEPS = {"y": 4, "z": 1}


def contract(left, right, left_dim, right_dim):
    return lax.dot_general(
        left, right, (((left_dim,), (right_dim,)), ((), ())), preferred_element_type=F32
    )


def lookup_kernel(high_ref, low_ref, table_ref, counts_ref, embeds_ref):
    groups = high_ref.shape[0]
    slot = lax.broadcasted_iota(jnp.int32, (256, 128), 0)

    def step(g, carry):
        left = jnp.where(slot == high_ref[pl.ds(g, 1), :], 1.0, 0.0).astype(BF)
        right = jnp.where(slot == low_ref[pl.ds(g, 1), :], 1.0, 0.0).astype(BF)
        both = contract(left, right, 1, 1).astype(BF)
        for h in range(16):
            counts_ref[pl.ds(pl.multiple_of(g * 16, 16), 16), h * 256 : (h + 1) * 256] = both[
                h * 16 : (h + 1) * 16
            ]
        return carry

    lax.fori_loop(0, groups, step, 0, unroll=8)
    embeds_ref[...] = jnp.dot(
        counts_ref[...], table_ref[...], preferred_element_type=F32
    ).astype(BF)


def lookup(emb_table, feature_ids):
    samples, feats, pool = feature_ids.shape
    rows = samples * feats
    lanes = (
        feature_ids.reshape(samples, feats // 16, 16, pool)
        .transpose(0, 1, 3, 2)
        .reshape(rows // 16, 128)
    )
    high = (lanes // 256) * 16 + lax.broadcasted_iota(jnp.int32, lanes.shape, 1) % 16
    low = lanes % 256
    steps = 1
    return pl.pallas_call(
        lookup_kernel,
        grid=(steps,),
        in_specs=[
            pl.BlockSpec((rows // 16 // steps, 128), lambda i: (i, 0)),
            pl.BlockSpec((rows // 16 // steps, 128), lambda i: (i, 0)),
            pl.BlockSpec(emb_table.shape, lambda i: (0, 0)),
        ],
        out_specs=[
            pl.BlockSpec((rows // steps, emb_table.shape[0]), lambda i: (i, 0)),
            pl.BlockSpec((rows // steps, emb_table.shape[1]), lambda i: (i, 0)),
        ],
        out_shape=[
            jax.ShapeDtypeStruct((rows, emb_table.shape[0]), BF),
            jax.ShapeDtypeStruct((rows, emb_table.shape[1]), BF),
        ],
        cost_estimate=pl.CostEstimate(
            flops=4 * rows * emb_table.shape[0] * emb_table.shape[1],
            bytes_accessed=2 * rows * emb_table.shape[0] + 4 * emb_table.size,
            transcendentals=0,
        ),
        name="lookup",
    )(high, low, emb_table)


def exchange(values, axis):
    return lax.all_to_all(values, axis, 0, 0)


def place(part):
    batch = lax.axis_index("batch")
    return batch // 4 if part == "y" else batch % 4


def swap(values, part, offset):
    pairs = [(b, b ^ (STEPS[part] * offset)) for b in range(16)]
    return lax.ppermute(values, "batch", pairs)


def sum_scattered(values, part):
    mine = place(part)
    take = lambda i: lax.dynamic_index_in_dim(values, i, 0, keepdims=False)
    came = [swap(take(mine ^ k), part, k) for k in (1, 2, 3)]
    return sum((c.astype(F32) for c in came), take(mine).astype(F32))


def sum_all(values, part):
    came = [swap(values, part, k) for k in (1, 2, 3)]
    return sum((c.astype(F32) for c in came), values.astype(F32)).astype(BF)


def gathered(values, axis, size):
    return exchange(jnp.broadcast_to(values[None], (size,) + values.shape), axis)


CHUNK = 256


def sample_kernel(
    which,
    x_ref,
    proj_ref,
    grad_ref,
    gain_ref,
    gate_ref,
    up_ref,
    down_ref,
    embed_ref,
    scaled_ref,
    gate_grad_ref,
    up_grad_ref,
    hidden_ref,
    inter_grad_ref,
    gain_grad_ref,
    interact_grad_ref,
):
    inter_map = contract(x_ref[...], proj_ref[...], 0, 0).astype(BF)
    gain_grad_ref[...] = jnp.zeros_like(gain_grad_ref)

    def step(i, carry):
        rows = pl.ds(pl.multiple_of(i * CHUNK, CHUNK), CHUNK)
        interact = jnp.dot(x_ref[rows, :], inter_map, preferred_element_type=F32)
        inv_rms = lax.rsqrt(jnp.mean(interact * interact, axis=-1, keepdims=True) + epsilon)
        normed = interact * inv_rms
        scaled = (normed * gain_ref[...]).astype(BF)
        scaled_ref[rows, :] = scaled
        scaled_grad = jnp.zeros((CHUNK, scaled.shape[1]), F32)
        for h in range(2):
            cols = slice(h * 256, (h + 1) * 256)
            gate_pre = jnp.dot(scaled, gate_ref[:, cols], preferred_element_type=F32)
            up_pre = jnp.dot(scaled, up_ref[:, cols], preferred_element_type=F32)
            hidden_grad = contract(grad_ref[which, rows, :], down_ref[cols, :], 1, 1)
            sigmoid = 1.0 / (1.0 + jnp.exp(-gate_pre))
            silu = gate_pre * sigmoid
            hidden_ref[rows, cols] = (silu * up_pre).astype(BF)
            up_grad = (hidden_grad * silu).astype(BF)
            up_grad_ref[rows, cols] = up_grad
            gate_grad = (
                hidden_grad * up_pre * sigmoid * (1.0 + gate_pre * (1.0 - sigmoid))
            ).astype(BF)
            gate_grad_ref[rows, cols] = gate_grad
            scaled_grad += contract(gate_grad, gate_ref[:, cols], 1, 1)
            scaled_grad += contract(up_grad, up_ref[:, cols], 1, 1)
        times_normed = scaled_grad * normed
        gain_grad_ref[...] += jnp.sum(times_normed.reshape(CHUNK // 8, 8, -1), axis=0)
        mean = jnp.mean(times_normed * gain_ref[...], axis=-1, keepdims=True)
        interact_grad_ref[rows, :] = (
            inv_rms * (scaled_grad * gain_ref[...] - normed * mean)
        ).astype(BF)
        return carry

    lax.fori_loop(0, x_ref.shape[0] // CHUNK, step, 0)
    inter_grad = contract(x_ref[...], interact_grad_ref[...], 0, 0).astype(BF)
    inter_grad_ref[...] = inter_grad
    embed_ref[...] = (
        contract(interact_grad_ref[...], inter_map, 1, 1) + contract(proj_ref[...], inter_grad, 1, 1)
    ).astype(BF)


def sample_pass(which, x, proj, out_grad, norm_gain, gate_weight, up_weight, down_weight):
    rows, width = x.shape
    hidden = gate_weight.shape[1]
    shape = jax.ShapeDtypeStruct
    return pl.pallas_call(
        functools.partial(sample_kernel, which),
        out_shape=[
            shape((rows, width), BF),
            shape((rows, width), BF),
            shape((rows, hidden), BF),
            shape((rows, hidden), BF),
            shape((rows, hidden), BF),
            shape((width, width), BF),
            shape((8, width), F32),
        ],
        in_specs=[pl.BlockSpec(memory_space=pltpu.VMEM)] * 7,
        out_specs=[pl.BlockSpec(memory_space=pltpu.VMEM)] * 7,
        scratch_shapes=[pltpu.VMEM((rows, width), BF)],
        cost_estimate=pl.CostEstimate(
            flops=9000000000, bytes_accessed=8 * rows * width * 2, transcendentals=rows * hidden
        ),
        compiler_params=pltpu.CompilerParams(vmem_limit_bytes=40 << 20),
        name="sample_pass",
    )(x, proj, out_grad, norm_gain[None], gate_weight, up_weight, down_weight)


def parts_kernel(*refs):
    (x0, x1, grads, down, s0, g0, u0, h0, z0, n0, s1, g1, u1, h1, z1, n1, out_ref, parts_ref) = refs

    def over(a0, b0, a1, b1):
        return contract(a0[...], b0[...], 0, 0) + contract(a1[...], b1[...], 0, 0)

    for at, part in ((0, over(s0, g0, s1, g1)), (32, over(s0, u0, s1, u1))):
        part = part.astype(BF).reshape(16, 16, 512)
        parts_ref[:, at : at + 16, :] = part[:, :, :256]
        parts_ref[:, at + 16 : at + 32, :] = part[:, :, 256:]
    part = over(h0, grads.at[0], h1, grads.at[1]).astype(BF)
    parts_ref[:, 64:96, :] = part.reshape(16, 32, 256)
    part = jnp.dot(x0[...], z0[...], preferred_element_type=F32) + jnp.dot(
        x1[...], z1[...], preferred_element_type=F32
    )
    parts_ref[:, 96:160, :] = part.astype(BF).reshape(16, 64, 256)
    part = jnp.sum(n0[...] + n1[...], axis=0, keepdims=True)
    parts_ref[:, 160:176, :] = jnp.broadcast_to(part[None], (16, 16, 256)).astype(BF)
    for s, hidden in enumerate((h0, h1)):
        out_ref[s] = jnp.dot(hidden[...], down[...], preferred_element_type=F32).astype(BF)


def parts_of(xs, out_grad, down_weight, passes):
    saved = [v for p in passes for v in p[1:]]
    return pl.pallas_call(
        parts_kernel,
        out_shape=[
            jax.ShapeDtypeStruct(out_grad.shape, BF),
            jax.ShapeDtypeStruct((16, 176, out_grad.shape[2]), BF),
        ],
        in_specs=[pl.BlockSpec(memory_space=pltpu.VMEM)] * (4 + len(saved)),
        out_specs=[pl.BlockSpec(memory_space=pltpu.VMEM)] * 2,
        cost_estimate=pl.CostEstimate(
            flops=6000000000, bytes_accessed=16000000, transcendentals=0
        ),
        compiler_params=pltpu.CompilerParams(vmem_limit_bytes=40 << 20),
        name="parts",
    )(*xs, out_grad, down_weight, *saved)


def per_device(
    emb_table, feature_ids, projection, norm_gain, gate_weight, up_weight, down_weight, out_grad
):
    samples, feats, pool = feature_ids.shape
    shards = 16
    own = samples // shards
    width = emb_table.shape[1]
    rank = projection.shape[1]
    all_feats = shards * feats
    proj = gathered(projection, "table", shards).reshape(all_feats, rank)
    ids = feature_ids.reshape(shards, own, feats, pool)
    counts, xs, passes, backs = [], [], [], []
    for c in range(own):
        count, embeds = lookup(emb_table, ids[:, c])
        if c == 0:
            embeds, proj = lax.optimization_barrier((embeds, proj))
        x = exchange(embeds.reshape(shards, feats, width), "table")
        counts.append(count)
        xs.append(x.reshape(all_feats, width))
        passes.append(
            sample_pass(c, xs[c], proj, out_grad, norm_gain, gate_weight, up_weight, down_weight)
        )
        back = exchange(passes[c][0].reshape(shards, feats, width), "table")
        backs.append(back.reshape(-1, width))

    block_out, parts = parts_of(xs, out_grad, down_weight, passes)
    parts, backs[-1] = lax.optimization_barrier((parts, backs[-1]))
    parts = exchange(parts, "table")
    parts = jnp.sum(parts.astype(F32), axis=0).astype(BF)
    parts = sum_all(parts, "z")
    parts = sum_all(parts, "y")
    projection_grad = parts[96:160].astype(F32)
    gain_grad = parts[160].astype(F32)
    weights = gathered(parts[:96], "table", shards)
    weights = weights.astype(F32)

    def joined(piece):
        return (
            piece.reshape(shards, 2, rank // shards, hidden_width // 2)
            .transpose(0, 2, 1, 3)
            .reshape(rank, hidden_width)
        )

    hidden_width = gate_weight.shape[1]
    gate_grad = joined(weights[:, :32])
    up_grad = joined(weights[:, 32:64])
    down_grad = weights[:, 64:96].reshape(hidden_width, width)

    table_term = contract(counts[0], backs[0], 0, 0)
    for c in range(1, own):
        table_term = table_term + contract(counts[c], backs[c], 0, 0)
    table_term = table_term.astype(BF)
    here = table_term.shape[0] // 16
    table_term = sum_scattered(table_term.reshape(4, 4 * here, width), "y").astype(BF)
    table_grad = sum_scattered(table_term.reshape(4, here, width), "z")
    return (block_out, table_grad, projection_grad, gain_grad, gate_grad, up_grad, down_grad)


def solution(mesh):
    return jax.shard_map(
        per_device,
        mesh=mesh,
        in_specs=(
            P("table", None),
            P("batch", "table", None),
            P("table", None),
            P(),
            P(),
            P(),
            P(),
            P(("batch", "table"), None, None),
        ),
        out_specs=(
            P(("batch", "table"), None, None),
            P(("table", "batch"), None),
            P("table", None),
            P(),
            P(),
            P(),
            P(),
        ),
        check_vma=False,
    )
```

```python
import functools

import jax
import jax.numpy as jnp
from jax import lax
from jax.experimental import pallas as pl
from jax.experimental.pallas import tpu as pltpu
from jax.sharding import PartitionSpec as P

epsilon = 1e-06
BF = jnp.bfloat16
F32 = jnp.float32
STEPS = {"y": 4, "z": 1}


def contract(left, right, left_dim, right_dim):
    return lax.dot_general(
        left, right, (((left_dim,), (right_dim,)), ((), ())), preferred_element_type=F32
    )


def lookup_kernel(high_ref, low_ref, table_ref, counts_ref, embeds_ref):
    groups = high_ref.shape[0]
    slot = lax.broadcasted_iota(jnp.int32, (256, 128), 0)

    def step(g, carry):
        left = jnp.where(slot == high_ref[pl.ds(g, 1), :], 1.0, 0.0).astype(BF)
        right = jnp.where(slot == low_ref[pl.ds(g, 1), :], 1.0, 0.0).astype(BF)
        both = contract(left, right, 1, 1).astype(BF)
        for h in range(16):
            counts_ref[pl.ds(pl.multiple_of(g * 16, 16), 16), h * 256 : (h + 1) * 256] = both[
                h * 16 : (h + 1) * 16
            ]
        return carry

    lax.fori_loop(0, groups, step, 0, unroll=8)
    embeds_ref[...] = jnp.dot(
        counts_ref[...], table_ref[...], preferred_element_type=F32
    ).astype(BF)


def lookup(emb_table, feature_ids):
    samples, feats, pool = feature_ids.shape
    rows = samples * feats
    lanes = (
        feature_ids.reshape(samples, feats // 16, 16, pool)
        .transpose(0, 1, 3, 2)
        .reshape(rows // 16, 128)
    )
    high = (lanes // 256) * 16 + lax.broadcasted_iota(jnp.int32, lanes.shape, 1) % 16
    low = lanes % 256
    steps = 1
    return pl.pallas_call(
        lookup_kernel,
        grid=(steps,),
        in_specs=[
            pl.BlockSpec((rows // 16 // steps, 128), lambda i: (i, 0)),
            pl.BlockSpec((rows // 16 // steps, 128), lambda i: (i, 0)),
            pl.BlockSpec(emb_table.shape, lambda i: (0, 0)),
        ],
        out_specs=[
            pl.BlockSpec((rows // steps, emb_table.shape[0]), lambda i: (i, 0)),
            pl.BlockSpec((rows // steps, emb_table.shape[1]), lambda i: (i, 0)),
        ],
        out_shape=[
            jax.ShapeDtypeStruct((rows, emb_table.shape[0]), BF),
            jax.ShapeDtypeStruct((rows, emb_table.shape[1]), BF),
        ],
        cost_estimate=pl.CostEstimate(
            flops=4 * rows * emb_table.shape[0] * emb_table.shape[1],
            bytes_accessed=2 * rows * emb_table.shape[0] + 4 * emb_table.size,
            transcendentals=0,
        ),
        name="lookup",
    )(high, low, emb_table)


def exchange(values, axis):
    return lax.all_to_all(values, axis, 0, 0)


def place(part):
    batch = lax.axis_index("batch")
    return batch // 4 if part == "y" else batch % 4


def swap(values, part, offset):
    pairs = [(b, b ^ (STEPS[part] * offset)) for b in range(16)]
    return lax.ppermute(values, "batch", pairs)


def sum_scattered(values, part):
    mine = place(part)
    take = lambda i: lax.dynamic_index_in_dim(values, i, 0, keepdims=False)
    came = [swap(take(mine ^ k), part, k) for k in (1, 2, 3)]
    return sum((c.astype(F32) for c in came), take(mine).astype(F32))


def sum_all(values, part):
    came = [swap(values, part, k) for k in (1, 2, 3)]
    return sum((c.astype(F32) for c in came), values.astype(F32)).astype(BF)


def gathered(values, axis, size):
    return exchange(jnp.broadcast_to(values[None], (size,) + values.shape), axis)


CHUNK = 256


def sample_kernel(which, *refs):
    (x_ref, proj_ref, grad_ref, gain_ref, gate_ref, up_ref, down_ref), refs = refs[:7], refs[7:]
    before, refs = (refs[:6], refs[6:]) if which else (None, refs)
    embed_ref, out_ref, *sums, scaled_ref, gate_grad_ref, up_grad_ref, hidden_ref = refs[:-2]
    interact_grad_ref, gain_sum_ref = refs[-2:]
    inter_map = contract(x_ref[...], proj_ref[...], 0, 0).astype(BF)
    gain_sum_ref[...] = before[5][...] if which else jnp.zeros_like(gain_sum_ref)

    def step(i, carry):
        rows = pl.ds(pl.multiple_of(i * CHUNK, CHUNK), CHUNK)
        interact = jnp.dot(x_ref[rows, :], inter_map, preferred_element_type=F32)
        inv_rms = lax.rsqrt(jnp.mean(interact * interact, axis=-1, keepdims=True) + epsilon)
        normed = interact * inv_rms
        scaled = (normed * gain_ref[...]).astype(BF)
        scaled_ref[rows, :] = scaled
        scaled_grad = jnp.zeros((CHUNK, scaled.shape[1]), F32)
        for h in range(2):
            cols = slice(h * 256, (h + 1) * 256)
            gate_pre = jnp.dot(scaled, gate_ref[:, cols], preferred_element_type=F32)
            up_pre = jnp.dot(scaled, up_ref[:, cols], preferred_element_type=F32)
            hidden_grad = contract(grad_ref[which, rows, :], down_ref[cols, :], 1, 1)
            sigmoid = 1.0 / (1.0 + jnp.exp(-gate_pre))
            silu = gate_pre * sigmoid
            hidden_ref[rows, cols] = (silu * up_pre).astype(BF)
            up_grad = (hidden_grad * silu).astype(BF)
            up_grad_ref[rows, cols] = up_grad
            gate_grad = (
                hidden_grad * up_pre * sigmoid * (1.0 + gate_pre * (1.0 - sigmoid))
            ).astype(BF)
            gate_grad_ref[rows, cols] = gate_grad
            scaled_grad += contract(gate_grad, gate_ref[:, cols], 1, 1)
            scaled_grad += contract(up_grad, up_ref[:, cols], 1, 1)
        times_normed = scaled_grad * normed
        gain_sum_ref[...] += jnp.sum(times_normed.reshape(CHUNK // 8, 8, -1), axis=0)
        mean = jnp.mean(times_normed * gain_ref[...], axis=-1, keepdims=True)
        interact_grad_ref[rows, :] = (
            inv_rms * (scaled_grad * gain_ref[...] - normed * mean)
        ).astype(BF)
        return carry

    lax.fori_loop(0, x_ref.shape[0] // CHUNK, step, 0)
    inter_grad = contract(x_ref[...], interact_grad_ref[...], 0, 0).astype(BF)
    embed_ref[...] = (
        contract(interact_grad_ref[...], inter_map, 1, 1) + contract(proj_ref[...], inter_grad, 1, 1)
    ).astype(BF)
    out = jnp.dot(hidden_ref[...], down_ref[...], preferred_element_type=F32).astype(BF)
    gate_part = contract(scaled_ref[...], gate_grad_ref[...], 0, 0)
    up_part = contract(scaled_ref[...], up_grad_ref[...], 0, 0)
    down_part = contract(hidden_ref[...], grad_ref[which], 0, 0)
    proj_part = jnp.dot(x_ref[...], inter_grad, preferred_element_type=F32)
    if not which:
        out_ref[...] = out
        for ref, part in zip(sums, (gate_part, up_part, down_part, proj_part)):
            ref[...] = part
        sums[4][...] = gain_sum_ref[...]
        return
    out_ref[0] = before[0][...]
    out_ref[1] = out
    (parts_ref,) = sums

    def put(at, part):
        piece = part.astype(BF)
        size = piece.shape[0] // 16
        for t in range(16):
            parts_ref[t % 2, t // 2, at : at + size, :] = piece[t * size : (t + 1) * size]

    for at, part in ((0, gate_part + before[1][...]), (32, up_part + before[2][...])):
        put(at, part[:, :256])
        put(at + 16, part[:, 256:])
    put(64, down_part + before[3][...])
    put(96, proj_part + before[4][...])
    gain = jnp.sum(gain_sum_ref[...], axis=0, keepdims=True)
    put(160, jnp.broadcast_to(gain, (256, gain.shape[1])))


def sample_pass(which, x, proj, out_grad, norm_gain, gate_weight, up_weight, down_weight, before):
    rows, width = x.shape
    hidden = gate_weight.shape[1]
    shape = jax.ShapeDtypeStruct
    if which:
        after = [shape(out_grad.shape, BF), shape((2, 8, 176, width), BF)]
    else:
        after = [
            shape((rows, width), BF),
            shape((width, hidden), F32),
            shape((width, hidden), F32),
            shape((hidden, width), F32),
            shape((rows, width), F32),
            shape((8, width), F32),
        ]
    return pl.pallas_call(
        functools.partial(sample_kernel, which),
        out_shape=[shape((rows, width), BF)] + after,
        in_specs=[pl.BlockSpec(memory_space=pltpu.VMEM)] * (7 + len(before)),
        out_specs=[pl.BlockSpec(memory_space=pltpu.VMEM)] * (1 + len(after)),
        scratch_shapes=[
            pltpu.VMEM((rows, width), BF),
            pltpu.VMEM((rows, hidden), BF),
            pltpu.VMEM((rows, hidden), BF),
            pltpu.VMEM((rows, hidden), BF),
            pltpu.VMEM((rows, width), BF),
            pltpu.VMEM((8, width), F32),
        ],
        cost_estimate=pl.CostEstimate(
            flops=10000000000, bytes_accessed=8 * rows * width * 2, transcendentals=rows * hidden
        ),
        name="sample_pass",
    )(x, proj, out_grad, norm_gain[None], gate_weight, up_weight, down_weight, *before)


def per_device(
    emb_table, feature_ids, projection, norm_gain, gate_weight, up_weight, down_weight, out_grad
):
    samples, feats, pool = feature_ids.shape
    shards = 16
    own = samples // shards
    width = emb_table.shape[1]
    rank = projection.shape[1]
    all_feats = shards * feats
    proj = gathered(projection, "table", shards).reshape(all_feats, rank)
    ids = feature_ids.reshape(shards, own, feats, pool)
    counts, backs, carried = [], [], ()
    for c in range(own):
        count, embeds = lookup(emb_table, ids[:, c])
        if c == 0:
            embeds, proj = lax.optimization_barrier((embeds, proj))
        x = exchange(embeds.reshape(shards, feats, width), "table")
        counts.append(count)
        embed_grad, *carried = sample_pass(
            c,
            x.reshape(all_feats, width),
            proj,
            out_grad,
            norm_gain,
            gate_weight,
            up_weight,
            down_weight,
            carried,
        )
        back = exchange(embed_grad.reshape(shards, feats, width), "table")
        backs.append(back.reshape(-1, width))

    block_out, parts = carried
    core = lax.axis_index("table") % 2
    take = lambda i: lax.dynamic_index_in_dim(parts, i, 0, keepdims=False)
    came = lax.ppermute(take(1 - core), "table", [(t, t ^ 1) for t in range(shards)])
    parts = (take(core).astype(F32) + came.astype(F32)).astype(BF)
    parts, backs[-1] = lax.optimization_barrier((parts, backs[-1]))
    parts = lax.all_to_all(
        parts, "table", 0, 0, axis_index_groups=[list(range(c, shards, 2)) for c in (0, 1)]
    )
    parts = jnp.sum(parts.astype(F32), axis=0).astype(BF)
    parts = sum_all(parts, "z")
    parts = sum_all(parts, "y")
    projection_grad = parts[96:160].astype(F32)
    gain_grad = parts[160].astype(F32)
    weights = gathered(parts[:96], "table", shards)
    weights = weights.astype(F32)

    def joined(piece):
        return (
            piece.reshape(shards, 2, rank // shards, hidden_width // 2)
            .transpose(0, 2, 1, 3)
            .reshape(rank, hidden_width)
        )

    hidden_width = gate_weight.shape[1]
    gate_grad = joined(weights[:, :32])
    up_grad = joined(weights[:, 32:64])
    down_grad = weights[:, 64:96].reshape(hidden_width, width)

    table_term = contract(counts[0], backs[0], 0, 0)
    for c in range(1, own):
        table_term = table_term + contract(counts[c], backs[c], 0, 0)
    table_term = table_term.astype(BF)
    here = table_term.shape[0] // 16
    table_term = sum_scattered(table_term.reshape(4, 4 * here, width), "y").astype(BF)
    table_grad = sum_scattered(table_term.reshape(4, here, width), "z")
    return (block_out, table_grad, projection_grad, gain_grad, gate_grad, up_grad, down_grad)


def solution(mesh):
    return jax.shard_map(
        per_device,
        mesh=mesh,
        in_specs=(
            P("table", None),
            P("batch", "table", None),
            P("table", None),
            P(),
            P(),
            P(),
            P(),
            P(("batch", "table"), None, None),
        ),
        out_specs=(
            P(("batch", "table"), None, None),
            P(("table", "batch"), None),
            P("table", None),
            P(),
            P(),
            P(),
            P(),
        ),
        check_vma=False,
    )
```

```python
import functools

import jax
import jax.numpy as jnp
from jax import lax
from jax.experimental import pallas as pl
from jax.experimental.pallas import tpu as pltpu
from jax.sharding import PartitionSpec as P

epsilon = 1e-06
BF = jnp.bfloat16
F32 = jnp.float32
STEPS = {"y": 4, "z": 1}
CHIPS = [list(range(c, 16, 2)) for c in (0, 1)]


def contract(left, right, left_dim, right_dim):
    return lax.dot_general(
        left, right, (((left_dim,), (right_dim,)), ((), ())), preferred_element_type=F32
    )


def lookup_kernel(high_ref, low_ref, table_ref, counts_ref, embeds_ref, held_ref, sems):
    segments = sems.shape[0]
    groups = high_ref.shape[0] // segments
    slot = lax.broadcasted_iota(jnp.int32, (256, 128), 0)

    def step(g, carry):
        left = jnp.where(slot == high_ref[pl.ds(g, 1), :], 1.0, 0.0).astype(BF)
        right = jnp.where(slot == low_ref[pl.ds(g, 1), :], 1.0, 0.0).astype(BF)
        both = contract(left, right, 1, 1).astype(BF)
        for h in range(16):
            held_ref[pl.ds(pl.multiple_of(g * 16, 16), 16), h * 256 : (h + 1) * 256] = both[
                h * 16 : (h + 1) * 16
            ]
        return carry

    def copy(i):
        rows = pl.ds(i * groups * 16, groups * 16)
        return pltpu.make_async_copy(held_ref.at[rows], counts_ref.at[rows], sems.at[i])

    for i in range(segments):
        lax.fori_loop(i * groups, (i + 1) * groups, step, 0, unroll=8)
        copy(i).start()
    embeds_ref[...] = jnp.dot(
        held_ref[...], table_ref[...], preferred_element_type=F32
    ).astype(BF)
    for i in range(segments):
        copy(i).wait()


def lookup(emb_table, feature_ids):
    samples, feats, pool = feature_ids.shape
    rows = samples * feats
    lanes = (
        feature_ids.reshape(samples, feats // 16, 16, pool)
        .transpose(0, 1, 3, 2)
        .reshape(rows // 16, 128)
    )
    high = (lanes // 256) * 16 + lax.broadcasted_iota(jnp.int32, lanes.shape, 1) % 16
    low = lanes % 256
    return pl.pallas_call(
        lookup_kernel,
        in_specs=[pl.BlockSpec(memory_space=pltpu.VMEM)] * 3,
        out_specs=[
            pl.BlockSpec(memory_space=pl.ANY),
            pl.BlockSpec(memory_space=pltpu.VMEM),
        ],
        out_shape=[
            jax.ShapeDtypeStruct((rows, emb_table.shape[0]), BF),
            jax.ShapeDtypeStruct((rows, emb_table.shape[1]), BF),
        ],
        scratch_shapes=[
            pltpu.VMEM((rows, emb_table.shape[0]), BF),
            pltpu.SemaphoreType.DMA((SEGMENTS,)),
        ],
        cost_estimate=pl.CostEstimate(
            flops=4 * rows * emb_table.shape[0] * emb_table.shape[1],
            bytes_accessed=2 * rows * emb_table.shape[0] + 4 * emb_table.size,
            transcendentals=0,
        ),
        name="lookup",
    )(high, low, emb_table)


def exchange(values, axis):
    return lax.all_to_all(values, axis, 0, 0)


def place(part):
    batch = lax.axis_index("batch")
    return batch // 4 if part == "y" else batch % 4


def swap(values, part, offset):
    pairs = [(b, b ^ (STEPS[part] * offset)) for b in range(16)]
    return lax.ppermute(values, "batch", pairs)


def sum_scattered(values, part):
    mine = place(part)
    take = lambda i: lax.dynamic_index_in_dim(values, i, 0, keepdims=False)
    came = [swap(take(mine ^ k), part, k) for k in (1, 2, 3)]
    return sum((c.astype(F32) for c in came), take(mine).astype(F32))


def sum_all(values, part):
    came = [swap(values, part, k) for k in (1, 2, 3)]
    return sum((c.astype(F32) for c in came), values.astype(F32)).astype(BF)


def gathered(values, axis, size):
    return exchange(jnp.broadcast_to(values[None], (size,) + values.shape), axis)


CHUNK = 256
SEGMENTS = 4


def sample_kernel(which, *refs):
    (x_ref, proj_ref, grad_ref, gain_ref, gate_ref, up_ref, down_ref), refs = refs[:7], refs[7:]
    before, refs = (refs[:6], refs[6:]) if which else (None, refs)
    embed_ref, out_ref, *sums, scaled_ref, gate_grad_ref, up_grad_ref, hidden_ref = refs[:-2]
    interact_grad_ref, gain_sum_ref = refs[-2:]
    inter_map = contract(x_ref[...], proj_ref[...], 0, 0).astype(BF)
    gain_sum_ref[...] = before[5][...] if which else jnp.zeros_like(gain_sum_ref)

    def step(i, carry):
        rows = pl.ds(pl.multiple_of(i * CHUNK, CHUNK), CHUNK)
        interact = jnp.dot(x_ref[rows, :], inter_map, preferred_element_type=F32)
        inv_rms = lax.rsqrt(jnp.mean(interact * interact, axis=-1, keepdims=True) + epsilon)
        normed = interact * inv_rms
        scaled = (normed * gain_ref[...]).astype(BF)
        scaled_ref[rows, :] = scaled
        scaled_grad = jnp.zeros((CHUNK, scaled.shape[1]), F32)
        for h in range(2):
            cols = slice(h * 256, (h + 1) * 256)
            gate_pre = jnp.dot(scaled, gate_ref[:, cols], preferred_element_type=F32)
            up_pre = jnp.dot(scaled, up_ref[:, cols], preferred_element_type=F32)
            hidden_grad = contract(grad_ref[which, rows, :], down_ref[cols, :], 1, 1)
            sigmoid = 1.0 / (1.0 + jnp.exp(-gate_pre))
            silu = gate_pre * sigmoid
            hidden_ref[rows, cols] = (silu * up_pre).astype(BF)
            up_grad = (hidden_grad * silu).astype(BF)
            up_grad_ref[rows, cols] = up_grad
            gate_grad = (
                hidden_grad * up_pre * sigmoid * (1.0 + gate_pre * (1.0 - sigmoid))
            ).astype(BF)
            gate_grad_ref[rows, cols] = gate_grad
            scaled_grad += contract(gate_grad, gate_ref[:, cols], 1, 1)
            scaled_grad += contract(up_grad, up_ref[:, cols], 1, 1)
        times_normed = scaled_grad * normed
        gain_sum_ref[...] += jnp.sum(times_normed.reshape(CHUNK // 8, 8, -1), axis=0)
        mean = jnp.mean(times_normed * gain_ref[...], axis=-1, keepdims=True)
        interact_grad_ref[rows, :] = (
            inv_rms * (scaled_grad * gain_ref[...] - normed * mean)
        ).astype(BF)
        return carry

    lax.fori_loop(0, x_ref.shape[0] // CHUNK, step, 0)
    inter_grad = contract(x_ref[...], interact_grad_ref[...], 0, 0).astype(BF)
    embed_ref[...] = (
        contract(interact_grad_ref[...], inter_map, 1, 1) + contract(proj_ref[...], inter_grad, 1, 1)
    ).astype(BF)
    out = jnp.dot(hidden_ref[...], down_ref[...], preferred_element_type=F32).astype(BF)
    gate_part = contract(scaled_ref[...], gate_grad_ref[...], 0, 0)
    up_part = contract(scaled_ref[...], up_grad_ref[...], 0, 0)
    down_part = contract(hidden_ref[...], grad_ref[which], 0, 0)
    proj_part = jnp.dot(x_ref[...], inter_grad, preferred_element_type=F32)
    if not which:
        out_ref[...] = out
        for ref, part in zip(sums, (gate_part, up_part, down_part, proj_part)):
            ref[...] = part
        sums[4][...] = gain_sum_ref[...]
        return
    out_ref[0] = before[0][...]
    out_ref[1] = out
    (parts_ref,) = sums

    def put(at, part):
        piece = part.astype(BF)
        size = piece.shape[0] // 16
        for t in range(16):
            parts_ref[t % 2, t // 2, at : at + size, :] = piece[t * size : (t + 1) * size]

    for at, part in ((0, gate_part + before[1][...]), (32, up_part + before[2][...])):
        put(at, part[:, :256])
        put(at + 16, part[:, 256:])
    put(64, down_part + before[3][...])
    put(96, proj_part + before[4][...])
    gain = jnp.sum(gain_sum_ref[...], axis=0, keepdims=True)
    put(160, jnp.broadcast_to(gain, (256, gain.shape[1])))


def sample_pass(which, x, proj, out_grad, norm_gain, gate_weight, up_weight, down_weight, before):
    rows, width = x.shape
    hidden = gate_weight.shape[1]
    shape = jax.ShapeDtypeStruct
    if which:
        after = [shape(out_grad.shape, BF), shape((2, 8, 176, width), BF)]
    else:
        after = [
            shape((rows, width), BF),
            shape((width, hidden), F32),
            shape((width, hidden), F32),
            shape((hidden, width), F32),
            shape((rows, width), F32),
            shape((8, width), F32),
        ]
    return pl.pallas_call(
        functools.partial(sample_kernel, which),
        out_shape=[shape((rows, width), BF)] + after,
        in_specs=[pl.BlockSpec(memory_space=pltpu.VMEM)] * (7 + len(before)),
        out_specs=[pl.BlockSpec(memory_space=pltpu.VMEM)] * (1 + len(after)),
        scratch_shapes=[
            pltpu.VMEM((rows, width), BF),
            pltpu.VMEM((rows, hidden), BF),
            pltpu.VMEM((rows, hidden), BF),
            pltpu.VMEM((rows, hidden), BF),
            pltpu.VMEM((rows, width), BF),
            pltpu.VMEM((8, width), F32),
        ],
        cost_estimate=pl.CostEstimate(
            flops=10000000000, bytes_accessed=8 * rows * width * 2, transcendentals=rows * hidden
        ),
        name="sample_pass",
    )(x, proj, out_grad, norm_gain[None], gate_weight, up_weight, down_weight, *before)


def finish_kernel(core_ref, mine_ref, other_ref, gate_ref, up_ref, down_ref):
    first = core_ref[0] == 0
    for t in range(16):
        own, swapped = mine_ref[t // 2], other_ref[t // 2]
        piece = jnp.where(first == (t % 2 == 0), own, swapped).astype(F32)
        rows = slice(t * 16, (t + 1) * 16)
        gate_ref[rows, :256], gate_ref[rows, 256:] = piece[:16], piece[16:32]
        up_ref[rows, :256], up_ref[rows, 256:] = piece[32:48], piece[48:64]
        down_ref[t * 32 : (t + 1) * 32, :] = piece[64:96]


def finish(core, mine, other, gate_shape, down_shape):
    return pl.pallas_call(
        finish_kernel,
        in_specs=[pl.BlockSpec(memory_space=pltpu.SMEM)]
        + [pl.BlockSpec(memory_space=pltpu.VMEM)] * 2,
        out_specs=[pl.BlockSpec(memory_space=pltpu.VMEM)] * 3,
        out_shape=[
            jax.ShapeDtypeStruct(gate_shape, F32),
            jax.ShapeDtypeStruct(gate_shape, F32),
            jax.ShapeDtypeStruct(down_shape, F32),
        ],
        name="finish",
    )(core[None], mine, other)


def per_device(
    emb_table, feature_ids, projection, norm_gain, gate_weight, up_weight, down_weight, out_grad
):
    samples, feats, pool = feature_ids.shape
    shards = 16
    own = samples // shards
    width = emb_table.shape[1]
    rank = projection.shape[1]
    all_feats = shards * feats
    proj = gathered(projection, "table", shards).reshape(all_feats, rank)
    ids = feature_ids.reshape(shards, own, feats, pool)
    counts, backs, carried = [], [], ()
    for c in range(own):
        count, embeds = lookup(emb_table, ids[:, c])
        if c == 0:
            embeds, proj = lax.optimization_barrier((embeds, proj))
        x = exchange(embeds.reshape(shards, feats, width), "table")
        counts.append(count)
        embed_grad, *carried = sample_pass(
            c,
            x.reshape(all_feats, width),
            proj,
            out_grad,
            norm_gain,
            gate_weight,
            up_weight,
            down_weight,
            carried,
        )
        back = exchange(embed_grad.reshape(shards, feats, width), "table")
        backs.append(back.reshape(-1, width))

    block_out, parts = carried
    core = lax.axis_index("table") % 2
    take = lambda i: lax.dynamic_index_in_dim(parts, i, 0, keepdims=False)
    came = lax.ppermute(take(1 - core), "table", [(t, t ^ 1) for t in range(shards)])
    parts = (take(core).astype(F32) + came.astype(F32)).astype(BF)
    parts, backs[-1] = lax.optimization_barrier((parts, backs[-1]))
    parts = lax.all_to_all(parts, "table", 0, 0, axis_index_groups=CHIPS)
    parts = jnp.sum(parts.astype(F32), axis=0).astype(BF)
    parts = sum_all(parts, "z")
    parts = sum_all(parts, "y")
    projection_grad = parts[96:160].astype(F32)
    gain_grad = parts[160].astype(F32)
    mine = lax.all_to_all(
        jnp.broadcast_to(parts[:96][None], (8, 96, width)),
        "table",
        0,
        0,
        axis_index_groups=CHIPS,
    )
    other = lax.ppermute(mine, "table", [(t, t ^ 1) for t in range(shards)])
    gate_grad, up_grad, down_grad = finish(core, mine, other, gate_weight.shape, down_weight.shape)

    table_term = contract(counts[0], backs[0], 0, 0)
    for c in range(1, own):
        table_term = table_term + contract(counts[c], backs[c], 0, 0)
    table_term = table_term.astype(BF)
    here = table_term.shape[0] // 16
    table_term = sum_scattered(table_term.reshape(4, 4 * here, width), "y").astype(BF)
    table_grad = sum_scattered(table_term.reshape(4, here, width), "z")
    return (block_out, table_grad, projection_grad, gain_grad, gate_grad, up_grad, down_grad)


def solution(mesh):
    return jax.shard_map(
        per_device,
        mesh=mesh,
        in_specs=(
            P("table", None),
            P("batch", "table", None),
            P("table", None),
            P(),
            P(),
            P(),
            P(),
            P(("batch", "table"), None, None),
        ),
        out_specs=(
            P(("batch", "table"), None, None),
            P(("table", "batch"), None),
            P("table", None),
            P(),
            P(),
            P(),
            P(),
        ),
        check_vma=False,
    )
```

```python
import functools

import jax
import jax.numpy as jnp
from jax import lax
from jax.experimental import pallas as pl
from jax.experimental.pallas import tpu as pltpu
from jax.sharding import PartitionSpec as P

epsilon = 1e-06
BF = jnp.bfloat16
F32 = jnp.float32
STEPS = {"y": 4, "z": 1}
CHIPS = [list(range(c, 16, 2)) for c in (0, 1)]


def contract(left, right, left_dim, right_dim):
    return lax.dot_general(
        left, right, (((left_dim,), (right_dim,)), ((), ())), preferred_element_type=F32
    )


def lookup_kernel(ids_ref, table_ref, counts_ref, embeds_ref, held_ref, sems):
    segments = sems.shape[0]
    groups = ids_ref.shape[0] // segments
    slot = lax.broadcasted_iota(jnp.int32, (256, 128), 0)
    lane = lax.broadcasted_iota(jnp.int32, (1, 128), 1) & 15

    def step(g, carry):
        ids = ids_ref[pl.ds(g, 1), :]
        left = jnp.where(slot == (ids >> 8) * 16 + lane, 1.0, 0.0).astype(BF)
        right = jnp.where(slot == (ids & 255), 1.0, 0.0).astype(BF)
        both = contract(left, right, 1, 1).astype(BF)
        for h in range(16):
            held_ref[pl.ds(pl.multiple_of(g * 16, 16), 16), h * 256 : (h + 1) * 256] = both[
                h * 16 : (h + 1) * 16
            ]
        return carry

    def copy(i):
        rows = pl.ds(i * groups * 16, groups * 16)
        return pltpu.make_async_copy(held_ref.at[rows], counts_ref.at[rows], sems.at[i])

    for i in range(segments):
        lax.fori_loop(i * groups, (i + 1) * groups, step, 0, unroll=8)
        copy(i).start()
    embeds_ref[...] = jnp.dot(
        held_ref[...], table_ref[...], preferred_element_type=F32
    ).astype(BF)
    for i in range(segments):
        copy(i).wait()


def lookup(emb_table, feature_ids):
    samples, feats, pool = feature_ids.shape
    rows = samples * feats
    lanes = (
        feature_ids.reshape(samples, feats // 16, 16, pool)
        .transpose(0, 1, 3, 2)
        .reshape(rows // 16, 128)
    )
    return pl.pallas_call(
        lookup_kernel,
        in_specs=[pl.BlockSpec(memory_space=pltpu.VMEM)] * 2,
        out_specs=[
            pl.BlockSpec(memory_space=pl.ANY),
            pl.BlockSpec(memory_space=pltpu.VMEM),
        ],
        out_shape=[
            jax.ShapeDtypeStruct((rows, emb_table.shape[0]), BF),
            jax.ShapeDtypeStruct((rows, emb_table.shape[1]), BF),
        ],
        scratch_shapes=[
            pltpu.VMEM((rows, emb_table.shape[0]), BF),
            pltpu.SemaphoreType.DMA((SEGMENTS,)),
        ],
        cost_estimate=pl.CostEstimate(
            flops=4 * rows * emb_table.shape[0] * emb_table.shape[1],
            bytes_accessed=2 * rows * emb_table.shape[0] + 4 * emb_table.size,
            transcendentals=0,
        ),
        name="lookup",
    )(lanes, emb_table)


def exchange(values, axis):
    return lax.all_to_all(values, axis, 0, 0)


def place(part):
    batch = lax.axis_index("batch")
    return batch // 4 if part == "y" else batch % 4


def swap(values, part, offset):
    pairs = [(b, b ^ (STEPS[part] * offset)) for b in range(16)]
    return lax.ppermute(values, "batch", pairs)


def sum_scattered(values, part):
    mine = place(part)
    take = lambda i: lax.dynamic_index_in_dim(values, i, 0, keepdims=False)
    came = [swap(take(mine ^ k), part, k) for k in (1, 2, 3)]
    return sum((c.astype(F32) for c in came), take(mine).astype(F32))


def sum_all(values, part):
    came = [swap(values, part, k) for k in (1, 2, 3)]
    return sum((c.astype(F32) for c in came), values.astype(F32)).astype(BF)


def gathered(values, axis, size):
    return exchange(jnp.broadcast_to(values[None], (size,) + values.shape), axis)


CHUNK = 512
SEGMENTS = 4


def sample_kernel(which, *refs):
    (x_ref, proj_ref, grad_ref, gain_ref, gate_ref, up_ref, down_ref), refs = refs[:7], refs[7:]
    before, refs = (refs[:6], refs[6:]) if which else (None, refs)
    embed_ref, out_ref, *sums, scaled_ref, gate_grad_ref, up_grad_ref, hidden_ref = refs[:-2]
    interact_grad_ref, gain_sum_ref = refs[-2:]
    inter_map = contract(x_ref[...], proj_ref[...], 0, 0).astype(BF)
    gain_sum_ref[...] = before[5][...] if which else jnp.zeros_like(gain_sum_ref)

    def step(i, carry):
        rows = pl.ds(pl.multiple_of(i * CHUNK, CHUNK), CHUNK)
        interact = jnp.dot(x_ref[rows, :], inter_map, preferred_element_type=F32)
        inv_rms = lax.rsqrt(jnp.mean(interact * interact, axis=-1, keepdims=True) + epsilon)
        normed = interact * inv_rms
        scaled = (normed * gain_ref[...]).astype(BF)
        scaled_ref[rows, :] = scaled
        scaled_grad = jnp.zeros((CHUNK, scaled.shape[1]), F32)
        for h in range(2):
            cols = slice(h * 256, (h + 1) * 256)
            gate_pre = jnp.dot(scaled, gate_ref[:, cols], preferred_element_type=F32)
            up_pre = jnp.dot(scaled, up_ref[:, cols], preferred_element_type=F32)
            hidden_grad = contract(grad_ref[which, rows, :], down_ref[cols, :], 1, 1)
            sigmoid = 1.0 / (1.0 + jnp.exp(-gate_pre))
            silu = gate_pre * sigmoid
            hidden_ref[rows, cols] = (silu * up_pre).astype(BF)
            up_grad = (hidden_grad * silu).astype(BF)
            up_grad_ref[rows, cols] = up_grad
            gate_grad = (
                hidden_grad * up_pre * sigmoid * (1.0 + gate_pre * (1.0 - sigmoid))
            ).astype(BF)
            gate_grad_ref[rows, cols] = gate_grad
            scaled_grad += contract(gate_grad, gate_ref[:, cols], 1, 1)
            scaled_grad += contract(up_grad, up_ref[:, cols], 1, 1)
        times_normed = scaled_grad * normed
        gain_sum_ref[...] += jnp.sum(times_normed.reshape(CHUNK // 8, 8, -1), axis=0)
        mean = jnp.mean(times_normed * gain_ref[...], axis=-1, keepdims=True)
        interact_grad_ref[rows, :] = (
            inv_rms * (scaled_grad * gain_ref[...] - normed * mean)
        ).astype(BF)
        return carry

    lax.fori_loop(0, x_ref.shape[0] // CHUNK, step, 0)
    inter_grad = contract(x_ref[...], interact_grad_ref[...], 0, 0).astype(BF)
    embed_ref[...] = (
        contract(interact_grad_ref[...], inter_map, 1, 1) + contract(proj_ref[...], inter_grad, 1, 1)
    ).astype(BF)
    out = jnp.dot(hidden_ref[...], down_ref[...], preferred_element_type=F32).astype(BF)
    gate_part = contract(scaled_ref[...], gate_grad_ref[...], 0, 0)
    up_part = contract(scaled_ref[...], up_grad_ref[...], 0, 0)
    down_part = contract(hidden_ref[...], grad_ref[which], 0, 0)
    proj_part = jnp.dot(x_ref[...], inter_grad, preferred_element_type=F32)
    if not which:
        out_ref[...] = out
        for ref, part in zip(sums, (gate_part, up_part, down_part, proj_part)):
            ref[...] = part
        sums[4][...] = gain_sum_ref[...]
        return
    out_ref[0] = before[0][...]
    out_ref[1] = out
    (parts_ref,) = sums

    def put(at, part):
        piece = part.astype(BF)
        size = piece.shape[0] // 16
        for t in range(16):
            parts_ref[t % 2, t // 2, at : at + size, :] = piece[t * size : (t + 1) * size]

    for at, part in ((0, gate_part + before[1][...]), (32, up_part + before[2][...])):
        put(at, part[:, :256])
        put(at + 16, part[:, 256:])
    put(64, down_part + before[3][...])
    put(96, proj_part + before[4][...])
    gain = jnp.sum(gain_sum_ref[...], axis=0, keepdims=True)
    put(160, jnp.broadcast_to(gain, (256, gain.shape[1])))


def sample_pass(which, x, proj, out_grad, norm_gain, gate_weight, up_weight, down_weight, before):
    rows, width = x.shape
    hidden = gate_weight.shape[1]
    shape = jax.ShapeDtypeStruct
    if which:
        after = [shape(out_grad.shape, BF), shape((2, 8, 176, width), BF)]
    else:
        after = [
            shape((rows, width), BF),
            shape((width, hidden), F32),
            shape((width, hidden), F32),
            shape((hidden, width), F32),
            shape((rows, width), F32),
            shape((8, width), F32),
        ]
    return pl.pallas_call(
        functools.partial(sample_kernel, which),
        out_shape=[shape((rows, width), BF)] + after,
        in_specs=[pl.BlockSpec(memory_space=pltpu.VMEM)] * (7 + len(before)),
        out_specs=[pl.BlockSpec(memory_space=pltpu.VMEM)] * (1 + len(after)),
        scratch_shapes=[
            pltpu.VMEM((rows, width), BF),
            pltpu.VMEM((rows, hidden), BF),
            pltpu.VMEM((rows, hidden), BF),
            pltpu.VMEM((rows, hidden), BF),
            pltpu.VMEM((rows, width), BF),
            pltpu.VMEM((8, width), F32),
        ],
        cost_estimate=pl.CostEstimate(
            flops=10000000000, bytes_accessed=8 * rows * width * 2, transcendentals=rows * hidden
        ),
        name="sample_pass",
    )(x, proj, out_grad, norm_gain[None], gate_weight, up_weight, down_weight, *before)


def quarter_kernel(_, counts0_ref, counts1_ref, back0_ref, back1_ref, out_ref, total_ref):
    term = jnp.dot(back0_ref[...].T, counts0_ref[...], preferred_element_type=F32)
    term += jnp.dot(back1_ref[...].T, counts1_ref[...], preferred_element_type=F32)
    step = pl.program_id(0)

    @pl.when(step == 0)
    def _():
        total_ref[...] = term

    @pl.when(step > 0)
    def _():
        total_ref[...] += term

    @pl.when(step == pl.num_programs(0) - 1)
    def _():
        out_ref[...] = total_ref[...].T.astype(BF)


def quarter(which, counts, backs):
    rows, width = backs[0].shape
    size = counts[0].shape[1] // 4
    steps = 2
    return pl.pallas_call(
        quarter_kernel,
        grid_spec=pltpu.PrefetchScalarGridSpec(
            num_scalar_prefetch=1,
            grid=(steps,),
            in_specs=[pl.BlockSpec((rows // steps, size), lambda i, w: (i, w[0]))] * 2
            + [pl.BlockSpec((rows // steps, width), lambda i, w: (i, 0))] * 2,
            out_specs=pl.BlockSpec((size, width), lambda i, w: (0, 0)),
            scratch_shapes=[pltpu.VMEM((width, size), F32)],
        ),
        out_shape=jax.ShapeDtypeStruct((size, width), BF),
        cost_estimate=pl.CostEstimate(
            flops=4 * rows * size * width, bytes_accessed=4 * rows * size, transcendentals=0
        ),
        name="quarter",
    )(which[None], *counts, *backs)


def finish_kernel(core_ref, mine_ref, other_ref, gate_ref, up_ref, down_ref):
    first = core_ref[0] == 0
    for t in range(16):
        own, swapped = mine_ref[t // 2], other_ref[t // 2]
        piece = jnp.where(first == (t % 2 == 0), own, swapped).astype(F32)
        rows = slice(t * 16, (t + 1) * 16)
        gate_ref[rows, :256], gate_ref[rows, 256:] = piece[:16], piece[16:32]
        up_ref[rows, :256], up_ref[rows, 256:] = piece[32:48], piece[48:64]
        down_ref[t * 32 : (t + 1) * 32, :] = piece[64:96]


def finish(core, mine, other, gate_shape, down_shape):
    return pl.pallas_call(
        finish_kernel,
        in_specs=[pl.BlockSpec(memory_space=pltpu.SMEM)]
        + [pl.BlockSpec(memory_space=pltpu.VMEM)] * 2,
        out_specs=[pl.BlockSpec(memory_space=pltpu.VMEM)] * 3,
        out_shape=[
            jax.ShapeDtypeStruct(gate_shape, F32),
            jax.ShapeDtypeStruct(gate_shape, F32),
            jax.ShapeDtypeStruct(down_shape, F32),
        ],
        name="finish",
    )(core[None], mine, other)


def per_device(
    emb_table, feature_ids, projection, norm_gain, gate_weight, up_weight, down_weight, out_grad
):
    samples, feats, pool = feature_ids.shape
    shards = 16
    own = samples // shards
    width = emb_table.shape[1]
    rank = projection.shape[1]
    all_feats = shards * feats
    proj = gathered(projection, "table", shards).reshape(all_feats, rank)
    ids = feature_ids.reshape(shards, own, feats, pool)
    counts, backs, carried = [], [], ()
    for c in range(own):
        count, embeds = lookup(emb_table, ids[:, c])
        if c == 0:
            embeds, proj = lax.optimization_barrier((embeds, proj))
        x = exchange(embeds.reshape(shards, feats, width), "table")
        counts.append(count)
        embed_grad, *carried = sample_pass(
            c,
            x.reshape(all_feats, width),
            proj,
            out_grad,
            norm_gain,
            gate_weight,
            up_weight,
            down_weight,
            carried,
        )
        back = exchange(embed_grad.reshape(shards, feats, width), "table")
        backs.append(back.reshape(-1, width))

    block_out, parts = carried
    core = lax.axis_index("table") % 2
    take = lambda i: lax.dynamic_index_in_dim(parts, i, 0, keepdims=False)
    came = lax.ppermute(take(1 - core), "table", [(t, t ^ 1) for t in range(shards)])
    parts = (take(core).astype(F32) + came.astype(F32)).astype(BF)
    parts, backs[-1] = lax.optimization_barrier((parts, backs[-1]))
    parts = lax.all_to_all(parts, "table", 0, 0, axis_index_groups=CHIPS)
    parts = jnp.sum(parts.astype(F32), axis=0).astype(BF)
    parts = sum_all(parts, "z")
    parts = sum_all(parts, "y")
    projection_grad = parts[96:160].astype(F32)
    gain_grad = parts[160].astype(F32)
    mine = lax.all_to_all(
        jnp.broadcast_to(parts[:96][None], (8, 96, width)),
        "table",
        0,
        0,
        axis_index_groups=CHIPS,
    )
    other = lax.ppermute(mine, "table", [(t, t ^ 1) for t in range(shards)])
    gate_grad, up_grad, down_grad = finish(core, mine, other, gate_weight.shape, down_weight.shape)

    mine = place("y")
    came = []
    for k in (2, 1, 3):
        piece = quarter(mine ^ k, counts, backs)
        came.append(swap(piece, "y", k))
    piece = quarter(mine, counts, backs)
    table_term = sum((c.astype(F32) for c in came), piece.astype(F32)).astype(BF)
    here = table_term.shape[0] // 4
    table_grad = sum_scattered(table_term.reshape(4, here, width), "z")
    return (block_out, table_grad, projection_grad, gain_grad, gate_grad, up_grad, down_grad)


def solution(mesh):
    return jax.shard_map(
        per_device,
        mesh=mesh,
        in_specs=(
            P("table", None),
            P("batch", "table", None),
            P("table", None),
            P(),
            P(),
            P(),
            P(),
            P(("batch", "table"), None, None),
        ),
        out_specs=(
            P(("batch", "table"), None, None),
            P(("table", "batch"), None),
            P("table", None),
            P(),
            P(),
            P(),
            P(),
        ),
        check_vma=False,
    )
```
